128 devices in a mesh: mb: 4 (over y), feat: 32 (over z, x, core).
Axes of the slice: x: 4, y: 4, z: 4, core: 2. Of those that a mesh axis runs over, the one named last changes fastest.
Arguments:
- features: float32 [1024, 262144], P('feat', 'mb'), may hold values from -6 to 6
- tile_rows: int32 [768], P('mb'), may hold values from 0 to 127
- tile_cols: int32 [768], P('mb'), may hold values from 0 to 511
- tile_masks: int32 [768, 128, 128], P('mb'), may hold values 0 or 1
- weight: bfloat16 [1024, 256], replicated, may hold values from -0.5625 to 0.5625
- upstream: bfloat16 [65536, 256], P(('mb', 'feat')), may hold values from -6 to 6
Outputs:
- activation: bfloat16 [65536, 256], P(('mb', 'feat'))
- weight_grad: float32 [1024, 256], P('feat')
The draws below stay inside these ranges and needn't reach their ends.
All inputs are finite; a program needn't handle non-finite values. No bound on the sum of `tile_masks` on one device may be relied on, other than what follows from the above.
Results may differ from the reference program's by a relative error of at most 0.0063.
Values may be sent and summed in bfloat16 or wider, within the bound.
No kernel may reach another device: no remote copies, remote signals or barrier semaphores. Data moves between devices by JAX's collectives and lax.ppermute only.
A program may use at most 128 MiB of HBM per device.

```python
import math
import jax
import jax.numpy as jnp
import numpy as np
from jax import lax

F = 1024
OUT = 256
TILE = 128
NT = 16384
NSRC = 65536
TILES = 192
SRC_ALL = 262144
TGT_ALL = 65536
TILES_ALL = 768
N_MB = 4


def plant(result, own_key, low, high):
    dims = result.shape
    place = [jax.random.randint(jax.random.fold_in(own_key, axis), (), 0, dims[axis]) for axis in range(len(dims))]
    result = result.at[tuple(place)].set(low)
    longest = dims.index(max(dims))
    place[longest] = (place[longest] + 1) % dims[longest]
    return result.at[tuple(place)].set(high)


def block_scale(own_key, extent, cuts, least, top_value):
    factor_of, own = 1.0, jax.random.fold_in(own_key, 6)
    for dim, shards_of in cuts:
        draws = jnp.exp(jax.random.uniform(jax.random.fold_in(own, dim), (shards_of,), jnp.float32, least / len(cuts), top_value / len(cuts)))
        factor_of = factor_of * jnp.repeat(draws, extent[dim] // shards_of).reshape([-1 if axis == dim else 1 for axis in range(len(extent))])
    return factor_of


def rank_bounds(count, skew):
    loads = [(1 << 20) // math.isqrt(grade ** skew) + 1 for grade in range(1, count + 1)]
    spread = 1 + sum(loads) // (1 << 30)
    return np.cumsum(np.array([max(1, weight // spread) for weight in loads]))


def skewed_ids(own_key, dims, count, slope):
    listing = rank_bounds(count, slope)
    pick = jax.random.randint(jax.random.fold_in(own_key, 1), dims, 0, int(listing[count - 1]))
    standing = jnp.searchsorted(jnp.asarray(listing, jnp.int32), pick, side="right")
    return jax.random.permutation(jax.random.fold_in(own_key, 2), count)[standing].astype(jnp.int32)


def normal_values(rng, extent, deviation, bound, cuts=(), held_as=jnp.bfloat16):
    drawn = deviation * jax.random.normal(rng, extent, jnp.float32)
    if cuts:
        drawn = drawn * block_scale(rng, extent, cuts, -0.22, 0.18)
    return jnp.clip(drawn, -bound, bound).astype(held_as)


def setup_inputs(seed: int = 0) -> dict:
    streams_of = jax.random.split(jax.random.key(seed), 7)
    return {
        "features": normal_values(streams_of[0], (F, SRC_ALL), 1.0, 6.0, ((0, 32), (1, 4)), jnp.float32),
        "tile_rows": plant(skewed_ids(streams_of[1], (TILES_ALL,), NT // TILE, 2), jax.random.fold_in(streams_of[1], 3), 0, (NT // TILE) - 1).astype(jnp.int32),
        "tile_cols": plant(jax.random.randint(streams_of[2], (TILES_ALL,), 0, NSRC // TILE), jax.random.fold_in(streams_of[2], 1), 0, (NSRC // TILE) - 1).astype(jnp.int32),
        "tile_masks": plant((jax.random.randint(streams_of[3], (TILES_ALL, TILE, TILE), 0, 16) < 1).astype(jnp.int32), jax.random.fold_in(streams_of[3], 1), 0, 1),
        "weight": normal_values(streams_of[4], (F, OUT), (3.0 / F ** 0.5), 0.5625),
        "upstream": normal_values(streams_of[5], (TGT_ALL, OUT), 1.0, 6.0, ((0, 128),)),
    }


def smooth_gate(values):
    return 0.5 * values * (1.0 + lax.erf(values * 0.7071067811865476))


def gate_slope(values):
    return 0.5 * (1.0 + lax.erf(values * 0.7071067811865476)) + values * jnp.exp(-0.5 * values * values) * 0.3989422804014327


def neighbor_mean(sources, row_index, col_index, masks):
    feat_cols = sources.shape[0]
    src_count = sources.shape[1]
    tile_size = masks.shape[1]
    row_tiles = NT // tile_size
    blocks = sources.reshape(feat_cols, src_count // tile_size, tile_size)
    picked = jnp.take(blocks, col_index, axis=1)
    weights = masks.astype(jnp.float32)
    contrib = jnp.einsum("fts,tds->tfd", picked, weights, precision=lax.Precision.HIGHEST)
    onehot = (row_index[None, :] == jnp.arange(row_tiles, dtype=jnp.int32)[:, None]).astype(jnp.float32)
    summed = jnp.einsum("rt,tfd->frd", onehot, contrib, precision=lax.Precision.HIGHEST).reshape(feat_cols, NT)
    degree = jnp.dot(onehot, jnp.sum(weights, axis=2), precision=lax.Precision.HIGHEST).reshape(NT)
    return ((sources[:, :NT] + summed) / (degree[None, :] + 1.0)).astype(jnp.bfloat16)


def reference(features, tile_rows, tile_cols, tile_masks, weight, upstream):
    outputs = []
    grad_total = jnp.zeros((F, OUT), jnp.float32)
    for member in range(N_MB):
        sources = features[:, member * NSRC:(member + 1) * NSRC]
        first_tile = member * TILES
        hidden_t = neighbor_mean(sources, tile_rows[first_tile:first_tile + TILES], tile_cols[first_tile:first_tile + TILES], tile_masks[first_tile:first_tile + TILES])
        preact = lax.dot_general(hidden_t, weight, (((0,), (0,)), ((), ())), preferred_element_type=jnp.float32)
        outputs.append(smooth_gate(preact).astype(jnp.bfloat16))
        slopes = (upstream[member * NT:(member + 1) * NT].astype(jnp.float32) * gate_slope(preact)).astype(jnp.bfloat16)
        grad_total = grad_total + jnp.dot(hidden_t, slopes, preferred_element_type=jnp.float32)
    return jnp.concatenate(outputs, 0), grad_total
```

```python
import jax
import jax.numpy as jnp
from jax import lax
from jax.experimental import pallas as pl
from jax.experimental.pallas import tpu as pltpu
from jax.sharding import PartitionSpec as P

NT = 16384
TILE = 128
CHUNK = 16
AHEAD = 4


def aggregate_kernel(
    row_index,
    col_index,
    features,
    masks,
    hidden,
    rows,
    cols,
    total,
    degree,
    picked,
    mask_buf,
    index_sem,
    self_sem,
    pick_sem,
    mask_sem,
):
    feat_cols = features.shape[0]
    chunks = mask_buf.shape[0] // CHUNK
    peers, _, block = hidden.shape

    def mask_copy(chunk):
        span = pl.ds(chunk * CHUNK, CHUNK)
        return pltpu.make_async_copy(masks.at[span], mask_buf.at[span], mask_sem.at[chunk])

    def start_picks(chunk):
        for k in range(CHUNK):
            tile = chunk * CHUNK + k
            first = pl.multiple_of(cols[tile] * TILE, TILE)
            pltpu.make_async_copy(
                features.at[:, pl.ds(first, TILE)], picked.at[tile], pick_sem.at[chunk]
            ).start()

    fetch_rows = pltpu.make_async_copy(row_index, rows, index_sem.at[0])
    fetch_cols = pltpu.make_async_copy(col_index, cols, index_sem.at[1])
    own = pltpu.make_async_copy(features.at[:, pl.ds(0, NT)], total, self_sem)
    fetch_cols.start()
    fetch_rows.start()
    mask_copy(0).start()
    own.start()
    for chunk in range(1, AHEAD):
        mask_copy(chunk).start()
    fetch_cols.wait()
    for chunk in range(AHEAD):
        start_picks(chunk)
    fetch_rows.wait()
    degree[...] = jnp.zeros_like(degree)
    own.wait()
    ones = jnp.ones((16, TILE), jnp.bfloat16)

    def chunk_step(chunk, carry):
        @pl.when(chunk + AHEAD < chunks)
        def _():
            mask_copy(chunk + AHEAD).start()
            start_picks(chunk + AHEAD)

        span = pl.ds(chunk * CHUNK, CHUNK)
        mask_copy(chunk).wait()
        pltpu.make_async_copy(picked.at[span], picked.at[span], pick_sem.at[chunk]).wait()
        for k in range(CHUNK):
            tile = chunk * CHUNK + k
            values = picked[tile]
            high = values.astype(jnp.bfloat16)
            low = (values - high.astype(jnp.float32)).astype(jnp.bfloat16)
            stacked = jnp.concatenate([high, low, ones], axis=0)
            links = mask_buf[tile].astype(jnp.float32).astype(jnp.bfloat16)
            sums = lax.dot_general(
                stacked, links, (((1,), (1,)), ((), ())), preferred_element_type=jnp.float32
            )
            target = pl.ds(pl.multiple_of(rows[tile] * TILE, TILE), TILE)
            total[:, target] += sums[:feat_cols] + sums[feat_cols : 2 * feat_cols]
            degree[:, target] += sums[2 * feat_cols : 2 * feat_cols + 8]
        return carry

    lax.fori_loop(0, chunks, chunk_step, 0)

    def finish(peer, carry):
        span = pl.ds(pl.multiple_of(peer * block, block), block)
        scale = 1.0 / (degree[:, span] + 1.0)
        mean = total[:, span].reshape(feat_cols // 8, 8, block) * scale[None]
        hidden[peer] = mean.reshape(feat_cols, block).astype(jnp.bfloat16)
        return carry

    lax.fori_loop(0, peers, finish, 0)


def aggregate(features, tile_rows, tile_cols, tile_masks, peers):
    feat_cols = features.shape[0]
    tiles = tile_masks.shape[0]
    chunks = tiles // CHUNK
    return pl.pallas_call(
        aggregate_kernel,
        out_shape=jax.ShapeDtypeStruct((peers, feat_cols, NT // peers), jnp.bfloat16),
        in_specs=[
            pl.BlockSpec(memory_space=pltpu.HBM),
            pl.BlockSpec(memory_space=pltpu.HBM),
            pl.BlockSpec(memory_space=pltpu.HBM),
            pl.BlockSpec(memory_space=pltpu.HBM),
        ],
        out_specs=pl.BlockSpec(memory_space=pltpu.VMEM),
        scratch_shapes=[
            pltpu.SMEM((tiles,), jnp.int32),
            pltpu.SMEM((tiles,), jnp.int32),
            pltpu.VMEM((feat_cols, NT), jnp.float32),
            pltpu.VMEM((8, NT), jnp.float32),
            pltpu.VMEM((tiles, feat_cols, TILE), jnp.float32),
            pltpu.VMEM((tiles, TILE, TILE), jnp.int32),
            pltpu.SemaphoreType.DMA((2,)),
            pltpu.SemaphoreType.DMA,
            pltpu.SemaphoreType.DMA((chunks,)),
            pltpu.SemaphoreType.DMA((chunks,)),
        ],
        compiler_params=pltpu.CompilerParams(vmem_limit_bytes=32 << 20),
        name="aggregate",
    )(
        *(
            pltpu.with_memory_space_constraint(operand, pltpu.HBM)
            for operand in (tile_rows, tile_cols, features, tile_masks)
        )
    )


def layer_kernel(hidden, weight, upstream, activation, partial):
    peers, feat_cols, block = hidden.shape
    features = hidden[...].reshape(peers * feat_cols, block)
    preact = lax.dot_general(
        features, weight[...], (((0,), (0,)), ((), ())), preferred_element_type=jnp.float32
    )
    phi = 0.5 * (1.0 + lax.erf(preact * 0.7071067811865476))
    activation[...] = (preact * phi).astype(jnp.bfloat16)
    slope = phi + preact * jnp.exp(-0.5 * preact * preact) * 0.3989422804014327
    slopes = (upstream[...].astype(jnp.float32) * slope).astype(jnp.bfloat16)
    grad = jnp.dot(features, slopes, preferred_element_type=jnp.float32)
    partial[...] = grad.astype(jnp.bfloat16).reshape(partial.shape)


def layer(hidden, weight, upstream):
    peers, feat_cols, _ = hidden.shape
    out = weight.shape[1]
    return pl.pallas_call(
        layer_kernel,
        out_shape=(
            jax.ShapeDtypeStruct(upstream.shape, jnp.bfloat16),
            jax.ShapeDtypeStruct((peers, feat_cols, out), jnp.bfloat16),
        ),
        in_specs=[pl.BlockSpec(memory_space=pltpu.VMEM)] * 3,
        out_specs=[pl.BlockSpec(memory_space=pltpu.VMEM)] * 2,
        compiler_params=pltpu.CompilerParams(vmem_limit_bytes=32 << 20),
        name="layer",
    )(hidden, weight, upstream)


def per_device(features, tile_rows, tile_cols, tile_masks, weight, upstream):
    peers = weight.shape[0] // features.shape[0]
    hidden = aggregate(features, tile_rows, tile_cols, tile_masks, peers)
    hidden = lax.all_to_all(hidden, "feat", 0, 0)
    activation, partial = layer(hidden, weight, upstream)
    partial = lax.all_to_all(partial, "feat", 0, 0)
    local_grad = jnp.sum(partial.astype(jnp.float32), axis=0)
    weight_grad = lax.psum(local_grad, "mb")
    return (activation, weight_grad)


def solution(mesh):
    return jax.shard_map(
        per_device,
        mesh=mesh,
        in_specs=(
            P("feat", "mb"),
            P("mb"),
            P("mb"),
            P("mb", None, None),
            P(),
            P(("mb", "feat"), None),
        ),
        out_specs=(P(("mb", "feat"), None), P("feat", None)),
        check_vma=False,
    )
```

```python
import jax
import jax.numpy as jnp
from jax import lax
from jax.experimental import pallas as pl
from jax.experimental.pallas import tpu as pltpu
from jax.sharding import Mesh
from jax.sharding import PartitionSpec as P

NT = 16384
N_MB = 4
CORES = 2
FEAT = ("z", "x", "core")
TILE = 128
CHUNK = 32
AHEAD = 3
FINISH = 8


def aggregate_kernel(
    row_index,
    col_index,
    features,
    masks,
    hidden,
    rows,
    cols,
    own,
    total,
    degree,
    picked,
    mask_buf,
    index_sem,
    self_sem,
    pick_sem,
    mask_sem,
):
    feat_cols = features.shape[0]
    chunks = mask_buf.shape[0] // CHUNK
    peers, _, block = hidden.shape

    def mask_copy(chunk):
        span = pl.ds(chunk * CHUNK, CHUNK)
        return pltpu.make_async_copy(masks.at[span], mask_buf.at[span], mask_sem.at[chunk])

    def start_pick(chunk, k):
        tile = chunk * CHUNK + k
        first = pl.multiple_of(cols[tile] * TILE, TILE)
        pltpu.make_async_copy(
            features.at[:, pl.ds(first, TILE)], picked.at[tile], pick_sem.at[chunk]
        ).start()

    fetch_rows = pltpu.make_async_copy(row_index, rows, index_sem.at[0])
    fetch_cols = pltpu.make_async_copy(col_index, cols, index_sem.at[1])
    fetch_own = pltpu.make_async_copy(features.at[:, pl.ds(0, NT)], own, self_sem)
    fetch_cols.start()
    fetch_rows.start()
    mask_copy(0).start()
    total[...] = jnp.zeros_like(total)
    degree[...] = jnp.zeros_like(degree)
    fetch_cols.wait()
    fetch_rows.wait()
    for chunk in range(AHEAD):
        if chunk:
            mask_copy(chunk).start()
        for k in range(CHUNK):
            start_pick(chunk, k)
    fetch_own.start()
    counter = jnp.concatenate(
        [jnp.ones((16, TILE), jnp.bfloat16), jnp.zeros((16, TILE), jnp.bfloat16)], axis=1
    )

    def chunk_step(chunk, prefetch):
        span = pl.ds(chunk * CHUNK, CHUNK)
        if prefetch:
            mask_copy(chunk + AHEAD).start()
        mask_copy(chunk).wait()
        pltpu.make_async_copy(picked.at[span], picked.at[span], pick_sem.at[chunk]).wait()
        for k in range(CHUNK):
            if prefetch:
                start_pick(chunk + AHEAD, k)
            tile = chunk * CHUNK + k
            values = picked[tile]
            high = values.astype(jnp.bfloat16)
            low = (values - high.astype(jnp.float32)).astype(jnp.bfloat16)
            halves = jnp.concatenate([jnp.concatenate([high, low], axis=1), counter], axis=0)
            links = mask_buf[tile].astype(jnp.float32).astype(jnp.bfloat16).T
            sums = jnp.dot(
                halves,
                jnp.concatenate([links, links], axis=0),
                preferred_element_type=jnp.float32,
            )
            target = pl.ds(pl.multiple_of(rows[tile] * TILE, TILE), TILE)
            total[:, target] += sums[:feat_cols]
            degree[:, target] += sums[feat_cols : feat_cols + 8]

    @pl.loop(0, chunks - AHEAD)
    def _(chunk):
        chunk_step(chunk, True)

    @pl.loop(chunks - AHEAD, chunks)
    def _(chunk):
        chunk_step(chunk, False)

    fetch_own.wait()

    @pl.loop(0, peers // FINISH)
    def _(step):
        for k in range(FINISH):
            peer = step * FINISH + k
            span = pl.ds(pl.multiple_of(peer * block, block), block)
            scale = 1.0 / (degree[:, span] + 1.0)
            mean = (total[:, span] + own[:, span]).reshape(feat_cols // 8, 8, block) * scale[None]
            hidden[peer] = mean.reshape(feat_cols, block).astype(jnp.bfloat16)


def aggregate(features, tile_rows, tile_cols, tile_masks, peers):
    feat_cols = features.shape[0]
    tiles = tile_masks.shape[0]
    chunks = tiles // CHUNK
    return pl.pallas_call(
        aggregate_kernel,
        out_shape=jax.ShapeDtypeStruct((peers, feat_cols, NT // peers), jnp.bfloat16),
        in_specs=[
            pl.BlockSpec(memory_space=pltpu.HBM),
            pl.BlockSpec(memory_space=pltpu.HBM),
            pl.BlockSpec(memory_space=pltpu.HBM),
            pl.BlockSpec(memory_space=pltpu.HBM),
        ],
        out_specs=pl.BlockSpec(memory_space=pltpu.VMEM),
        scratch_shapes=[
            pltpu.SMEM((tiles,), jnp.int32),
            pltpu.SMEM((tiles,), jnp.int32),
            pltpu.VMEM((feat_cols, NT), jnp.float32),
            pltpu.VMEM((feat_cols, NT), jnp.float32),
            pltpu.VMEM((8, NT), jnp.float32),
            pltpu.VMEM((tiles, feat_cols, TILE), jnp.float32),
            pltpu.VMEM((tiles, TILE, TILE), jnp.int32),
            pltpu.SemaphoreType.DMA((2,)),
            pltpu.SemaphoreType.DMA,
            pltpu.SemaphoreType.DMA((chunks,)),
            pltpu.SemaphoreType.DMA((chunks,)),
        ],
        compiler_params=pltpu.CompilerParams(vmem_limit_bytes=32 << 20),
        name="aggregate",
    )(
        *(
            pltpu.with_memory_space_constraint(operand, pltpu.HBM)
            for operand in (tile_rows, tile_cols, features, tile_masks)
        )
    )


def layer_kernel(hidden, weight, upstream, activation, kept, sent):
    chips, cores, feat_cols, block = hidden.shape
    features = hidden[...].reshape(chips * cores * feat_cols, block)
    preact = lax.dot_general(
        features, weight[...], (((0,), (0,)), ((), ())), preferred_element_type=jnp.float32
    )
    phi = 0.5 * (1.0 + lax.erf(preact * 0.7071067811865476))
    activation[...] = (preact * phi).astype(jnp.bfloat16)
    slope = phi + preact * jnp.exp(-0.5 * preact * preact) * 0.3989422804014327
    slopes = (upstream[...].astype(jnp.float32) * slope).astype(jnp.bfloat16)
    core = lax.axis_index("core")
    for part, owner in ((sent, 1 - core), (kept, core)):
        rows = hidden[:, owner].reshape(chips * feat_cols, block)
        grad = jnp.dot(rows, slopes, preferred_element_type=jnp.float32)
        part[...] = grad.astype(part.dtype).reshape(part.shape)


def layer(hidden, weight, upstream):
    chips, cores, feat_cols, _ = hidden.shape
    out = weight.shape[1]
    return pl.pallas_call(
        layer_kernel,
        out_shape=(
            jax.ShapeDtypeStruct(upstream.shape, jnp.bfloat16),
            jax.ShapeDtypeStruct((chips, feat_cols, out), jnp.float32),
            jax.ShapeDtypeStruct((chips, feat_cols, out), jnp.bfloat16),
        ),
        in_specs=[pl.BlockSpec(memory_space=pltpu.VMEM)] * 3,
        out_specs=[pl.BlockSpec(memory_space=pltpu.VMEM)] * 3,
        compiler_params=pltpu.CompilerParams(vmem_limit_bytes=32 << 20),
        name="layer",
    )(hidden, weight, upstream)


def per_device(features, tile_rows, tile_cols, tile_masks, weight, upstream):
    peers = weight.shape[0] // features.shape[0]
    hidden = aggregate(features, tile_rows, tile_cols, tile_masks, peers)
    hidden = lax.all_to_all(hidden, FEAT, 0, 0)
    hidden = hidden.reshape(peers // CORES, CORES, *hidden.shape[1:])
    activation, kept, sent = layer(hidden, weight, upstream)
    partial = (kept + lax.ppermute(sent, "core", [(0, 1), (1, 0)])).astype(jnp.bfloat16)
    partial = lax.all_to_all(partial, ("z", "x"), 0, 0)
    local_grad = jnp.sum(partial.astype(jnp.float32), axis=0)
    weight_grad = local_grad
    for shift in range(1, N_MB):
        ring = [(member, (member + shift) % N_MB) for member in range(N_MB)]
        weight_grad += lax.ppermute(local_grad, "mb", ring)
    return (activation, weight_grad)


def solution(mesh):
    side = mesh.shape["feat"] // CORES
    side = int(side**0.5)
    mesh = Mesh(
        mesh.devices.reshape(mesh.shape["mb"], side, side, CORES), ("mb",) + FEAT
    )
    return jax.shard_map(
        per_device,
        mesh=mesh,
        in_specs=(
            P(FEAT, "mb"),
            P("mb"),
            P("mb"),
            P("mb", None, None),
            P(),
            P(("mb",) + FEAT, None),
        ),
        out_specs=(P(("mb",) + FEAT, None), P(FEAT, None)),
        check_vma=False,
    )
```

```python
import jax
import jax.numpy as jnp
from jax import lax
from jax.experimental import pallas as pl
from jax.experimental.pallas import tpu as pltpu
from jax.sharding import Mesh
from jax.sharding import PartitionSpec as P

NT = 16384
N_MB = 4
CORES = 2
FEAT = ("z", "x", "core")
TILE = 128
CHUNK = 32
AHEAD = 3
FINISH = 16


def aggregate_kernel(
    row_index,
    col_index,
    features,
    masks,
    hidden,
    rows,
    cols,
    own,
    total,
    degree,
    picked,
    mask_buf,
    index_sem,
    self_sem,
    pick_sem,
    mask_sem,
):
    feat_cols = features.shape[0]
    chunks = mask_buf.shape[0] // CHUNK
    peers, _, block = hidden.shape

    def mask_copy(chunk):
        span = pl.ds(chunk * CHUNK, CHUNK)
        return pltpu.make_async_copy(masks.at[span], mask_buf.at[span], mask_sem.at[chunk])

    def start_pick(chunk, k):
        tile = chunk * CHUNK + k
        first = pl.multiple_of(cols[tile] * TILE, TILE)
        pltpu.make_async_copy(
            features.at[:, pl.ds(first, TILE)], picked.at[tile], pick_sem.at[chunk]
        ).start()

    fetch_rows = pltpu.make_async_copy(row_index, rows, index_sem.at[0])
    fetch_cols = pltpu.make_async_copy(col_index, cols, index_sem.at[1])
    fetch_own = pltpu.make_async_copy(features.at[:, pl.ds(0, NT)], own, self_sem)
    fetch_cols.start()
    fetch_rows.start()
    mask_copy(0).start()
    mask_copy(1).start()
    total[...] = jnp.zeros_like(total)
    degree[...] = jnp.zeros_like(degree)
    fetch_cols.wait()
    fetch_rows.wait()
    for chunk in range(AHEAD):
        if chunk > 1:
            mask_copy(chunk).start()
        for k in range(CHUNK):
            start_pick(chunk, k)
    counter = jnp.concatenate(
        [jnp.ones((16, TILE), jnp.bfloat16), jnp.zeros((16, TILE), jnp.bfloat16)], axis=1
    )

    def chunk_step(chunk, prefetch):
        span = pl.ds(chunk * CHUNK, CHUNK)
        if prefetch:
            mask_copy(chunk + AHEAD).start()
        mask_copy(chunk).wait()
        pltpu.make_async_copy(picked.at[span], picked.at[span], pick_sem.at[chunk]).wait()
        for k in range(CHUNK):
            if prefetch:
                start_pick(chunk + AHEAD, k)
            tile = chunk * CHUNK + k
            values = picked[tile]
            high = values.astype(jnp.bfloat16)
            low = (values - high.astype(jnp.float32)).astype(jnp.bfloat16)
            halves = jnp.concatenate([jnp.concatenate([high, low], axis=1), counter], axis=0)
            links = mask_buf[tile].astype(jnp.float32).astype(jnp.bfloat16).T
            sums = jnp.dot(
                halves,
                jnp.concatenate([links, links], axis=0),
                preferred_element_type=jnp.float32,
            )
            target = pl.ds(pl.multiple_of(rows[tile] * TILE, TILE), TILE)
            total[:, target] += sums[:feat_cols]
            degree[:, target] += sums[feat_cols : feat_cols + 8]

    @pl.loop(0, chunks - AHEAD)
    def _(chunk):
        chunk_step(chunk, True)

    fetch_own.start()

    @pl.loop(chunks - AHEAD, chunks)
    def _(chunk):
        chunk_step(chunk, False)

    fetch_own.wait()

    @pl.loop(0, peers // FINISH)
    def _(step):
        for k in range(FINISH):
            peer = step * FINISH + k
            span = pl.ds(pl.multiple_of(peer * block, block), block)
            scale = 1.0 / (degree[:, span] + 1.0)
            mean = (total[:, span] + own[:, span]).reshape(feat_cols // 8, 8, block) * scale[None]
            hidden[peer] = mean.reshape(feat_cols, block).astype(jnp.bfloat16)


def aggregate(features, tile_rows, tile_cols, tile_masks, peers):
    feat_cols = features.shape[0]
    tiles = tile_masks.shape[0]
    chunks = tiles // CHUNK
    return pl.pallas_call(
        aggregate_kernel,
        out_shape=jax.ShapeDtypeStruct((peers, feat_cols, NT // peers), jnp.bfloat16),
        in_specs=[
            pl.BlockSpec(memory_space=pltpu.HBM),
            pl.BlockSpec(memory_space=pltpu.HBM),
            pl.BlockSpec(memory_space=pltpu.HBM),
            pl.BlockSpec(memory_space=pltpu.HBM),
        ],
        out_specs=pl.BlockSpec(memory_space=pltpu.VMEM),
        scratch_shapes=[
            pltpu.SMEM((tiles,), jnp.int32),
            pltpu.SMEM((tiles,), jnp.int32),
            pltpu.VMEM((feat_cols, NT), jnp.float32),
            pltpu.VMEM((feat_cols, NT), jnp.float32),
            pltpu.VMEM((8, NT), jnp.float32),
            pltpu.VMEM((tiles, feat_cols, TILE), jnp.float32),
            pltpu.VMEM((tiles, TILE, TILE), jnp.int32),
            pltpu.SemaphoreType.DMA((2,)),
            pltpu.SemaphoreType.DMA,
            pltpu.SemaphoreType.DMA((chunks,)),
            pltpu.SemaphoreType.DMA((chunks,)),
        ],
        compiler_params=pltpu.CompilerParams(vmem_limit_bytes=32 << 20),
        name="aggregate",
    )(
        *(
            pltpu.with_memory_space_constraint(operand, pltpu.HBM)
            for operand in (tile_rows, tile_cols, features, tile_masks)
        )
    )


def gate(preact):
    return 0.5 * (1.0 + lax.erf(preact * 0.7071067811865476))


def slopes_kernel(hidden, weight, upstream, preact, slopes, sent):
    chips, cores, feat_cols, block = hidden.shape
    for first in range(0, block, TILE):
        span = slice(first, first + TILE)
        features = hidden[:, :, :, span].reshape(chips * cores * feat_cols, TILE)
        value = jnp.dot(features.T, weight[...], preferred_element_type=jnp.float32)
        preact[span] = value
        slope = gate(value) + value * jnp.exp(-0.5 * value * value) * 0.3989422804014327
        slopes[span] = (upstream[span].astype(jnp.float32) * slope).astype(jnp.bfloat16)
    rows = hidden[:, 1 - lax.axis_index("core")].reshape(chips * feat_cols, block)
    grad = jnp.dot(rows, slopes[...], preferred_element_type=jnp.float32)
    sent[...] = grad.astype(jnp.bfloat16).reshape(sent.shape)


def rest_kernel(hidden, preact, slopes, activation, kept):
    chips, cores, feat_cols, block = hidden.shape
    rows = hidden[:, lax.axis_index("core")].reshape(chips * feat_cols, block)
    grad = jnp.dot(rows, slopes[...], preferred_element_type=jnp.float32)
    kept[...] = grad.reshape(kept.shape)
    activation[...] = (preact[...] * gate(preact[...])).astype(jnp.bfloat16)


def call_in_vmem(kernel, name, outputs, *operands):
    in_vmem = pl.BlockSpec(memory_space=pltpu.VMEM)
    return pl.pallas_call(
        kernel,
        out_shape=outputs,
        in_specs=[in_vmem] * len(operands),
        out_specs=[in_vmem] * len(outputs),
        compiler_params=pltpu.CompilerParams(vmem_limit_bytes=32 << 20),
        name=name,
    )(*operands)


def layer(hidden, weight, upstream):
    chips, cores, feat_cols, _ = hidden.shape
    grad_shape = (chips, feat_cols, weight.shape[1])
    preact, slopes, sent = call_in_vmem(
        slopes_kernel,
        "slopes",
        (
            jax.ShapeDtypeStruct(upstream.shape, jnp.float32),
            jax.ShapeDtypeStruct(upstream.shape, jnp.bfloat16),
            jax.ShapeDtypeStruct(grad_shape, jnp.bfloat16),
        ),
        hidden,
        weight,
        upstream,
    )
    received = lax.ppermute(sent, "core", [(0, 1), (1, 0)])
    activation, kept = call_in_vmem(
        rest_kernel,
        "rest",
        (
            jax.ShapeDtypeStruct(upstream.shape, jnp.bfloat16),
            jax.ShapeDtypeStruct(grad_shape, jnp.float32),
        ),
        hidden,
        preact,
        slopes,
    )
    return activation, (kept + received).astype(jnp.bfloat16)


def per_device(features, tile_rows, tile_cols, tile_masks, weight, upstream):
    peers = weight.shape[0] // features.shape[0]
    hidden = aggregate(features, tile_rows, tile_cols, tile_masks, peers)
    hidden = lax.all_to_all(hidden, FEAT, 0, 0)
    hidden = hidden.reshape(peers // CORES, CORES, *hidden.shape[1:])
    activation, partial = layer(hidden, weight, upstream)
    partial = lax.all_to_all(partial, ("z", "x"), 0, 0)
    local_grad = jnp.sum(partial.astype(jnp.float32), axis=0)
    weight_grad = local_grad
    for shift in range(1, N_MB):
        ring = [(member, (member + shift) % N_MB) for member in range(N_MB)]
        weight_grad += lax.ppermute(local_grad, "mb", ring)
    return (activation, weight_grad)


def solution(mesh):
    side = mesh.shape["feat"] // CORES
    side = int(side**0.5)
    mesh = Mesh(
        mesh.devices.reshape(mesh.shape["mb"], side, side, CORES), ("mb",) + FEAT
    )
    return jax.shard_map(
        per_device,
        mesh=mesh,
        in_specs=(
            P(FEAT, "mb"),
            P("mb"),
            P("mb"),
            P("mb", None, None),
            P(),
            P(("mb",) + FEAT, None),
        ),
        out_specs=(P(("mb",) + FEAT, None), P(FEAT, None)),
        check_vma=False,
    )
```

```python
import jax
import jax.numpy as jnp
from jax import lax
from jax.experimental import pallas as pl
from jax.experimental.pallas import tpu as pltpu
from jax.sharding import Mesh
from jax.sharding import PartitionSpec as P

NT = 16384
N_MB = 4
CORES = 2
FEAT = ("z", "x", "core")
TILE = 128
CHUNK = 32
AHEAD = 3
FINISH = 8


def aggregate_kernel(
    row_index,
    col_index,
    features,
    masks,
    hidden,
    rows,
    cols,
    own,
    total,
    degree,
    picked,
    mask_buf,
    index_sem,
    self_sem,
    pick_sem,
    mask_sem,
):
    feat_cols = features.shape[0]
    chunks = mask_buf.shape[0] // CHUNK
    peers, _, block = hidden.shape

    def mask_copy(chunk):
        span = pl.ds(chunk * CHUNK, CHUNK)
        return pltpu.make_async_copy(masks.at[span], mask_buf.at[span], mask_sem.at[chunk])

    def start_pick(chunk, k):
        tile = chunk * CHUNK + k
        first = pl.multiple_of(cols[tile] * TILE, TILE)
        pltpu.make_async_copy(
            features.at[:, pl.ds(first, TILE)], picked.at[tile], pick_sem.at[chunk]
        ).start()

    fetch_rows = pltpu.make_async_copy(row_index, rows, index_sem.at[0])
    fetch_cols = pltpu.make_async_copy(col_index, cols, index_sem.at[1])

    def own_copy(part):
        span = pl.ds(part * (FINISH * block), FINISH * block)
        return pltpu.make_async_copy(features.at[:, span], own.at[:, span], self_sem.at[part])

    fetch_cols.start()
    fetch_rows.start()
    mask_copy(0).start()
    mask_copy(1).start()
    total[...] = jnp.zeros_like(total)
    degree[...] = jnp.zeros_like(degree)
    fetch_cols.wait()
    fetch_rows.wait()
    for chunk in range(AHEAD):
        if chunk > 1:
            mask_copy(chunk).start()
        for k in range(CHUNK):
            start_pick(chunk, k)
    counter = jnp.concatenate(
        [jnp.ones((16, TILE), jnp.bfloat16), jnp.zeros((16, TILE), jnp.bfloat16)], axis=1
    )

    def chunk_step(chunk, prefetch):
        span = pl.ds(chunk * CHUNK, CHUNK)
        if prefetch:
            mask_copy(chunk + AHEAD).start()
        mask_copy(chunk).wait()
        pltpu.make_async_copy(picked.at[span], picked.at[span], pick_sem.at[chunk]).wait()
        for k in range(CHUNK):
            if prefetch:
                start_pick(chunk + AHEAD, k)
            tile = chunk * CHUNK + k
            values = picked[tile]
            high = values.astype(jnp.bfloat16)
            low = (values - high.astype(jnp.float32)).astype(jnp.bfloat16)
            halves = jnp.concatenate([jnp.concatenate([high, low], axis=1), counter], axis=0)
            links = mask_buf[tile].astype(jnp.float32).astype(jnp.bfloat16).T
            sums = jnp.dot(
                halves,
                jnp.concatenate([links, links], axis=0),
                preferred_element_type=jnp.float32,
            )
            target = pl.ds(pl.multiple_of(rows[tile] * TILE, TILE), TILE)
            total[:, target] += sums[:feat_cols]
            degree[:, target] += sums[feat_cols : feat_cols + 8]

    @pl.loop(0, chunks - AHEAD)
    def _(chunk):
        chunk_step(chunk, True)

    for part in range(peers // FINISH):
        own_copy(part).start()

    @pl.loop(chunks - AHEAD, chunks)
    def _(chunk):
        chunk_step(chunk, False)

    @pl.loop(0, peers // FINISH)
    def _(step):
        own_copy(step).wait()
        for k in range(FINISH):
            peer = step * FINISH + k
            span = pl.ds(pl.multiple_of(peer * block, block), block)
            scale = 1.0 / (degree[:, span] + 1.0)
            mean = (total[:, span] + own[:, span]).reshape(feat_cols // 8, 8, block) * scale[None]
            hidden[peer] = mean.reshape(feat_cols, block).astype(jnp.bfloat16)


def aggregate(features, tile_rows, tile_cols, tile_masks, peers):
    feat_cols = features.shape[0]
    tiles = tile_masks.shape[0]
    chunks = tiles // CHUNK
    return pl.pallas_call(
        aggregate_kernel,
        out_shape=jax.ShapeDtypeStruct((peers, feat_cols, NT // peers), jnp.bfloat16),
        in_specs=[
            pl.BlockSpec(memory_space=pltpu.HBM),
            pl.BlockSpec(memory_space=pltpu.HBM),
            pl.BlockSpec(memory_space=pltpu.HBM),
            pl.BlockSpec(memory_space=pltpu.HBM),
        ],
        out_specs=pl.BlockSpec(memory_space=pltpu.VMEM),
        scratch_shapes=[
            pltpu.SMEM((tiles,), jnp.int32),
            pltpu.SMEM((tiles,), jnp.int32),
            pltpu.VMEM((feat_cols, NT), jnp.float32),
            pltpu.VMEM((feat_cols, NT), jnp.float32),
            pltpu.VMEM((8, NT), jnp.float32),
            pltpu.VMEM((tiles, feat_cols, TILE), jnp.float32),
            pltpu.VMEM((tiles, TILE, TILE), jnp.int32),
            pltpu.SemaphoreType.DMA((2,)),
            pltpu.SemaphoreType.DMA((peers // FINISH,)),
            pltpu.SemaphoreType.DMA((chunks,)),
            pltpu.SemaphoreType.DMA((chunks,)),
        ],
        compiler_params=pltpu.CompilerParams(vmem_limit_bytes=32 << 20),
        name="aggregate",
    )(
        *(
            pltpu.with_memory_space_constraint(operand, pltpu.HBM)
            for operand in (tile_rows, tile_cols, features, tile_masks)
        )
    )


def gate(preact):
    return 0.5 * (1.0 + lax.erf(preact * 0.7071067811865476))


def slopes_kernel(hidden, weight, upstream, preact, slopes, sent):
    chips, cores, feat_cols, block = hidden.shape
    for first in range(0, block, TILE):
        span = slice(first, first + TILE)
        features = hidden[:, :, :, span].reshape(chips * cores * feat_cols, TILE)
        value = jnp.dot(features.T, weight[...], preferred_element_type=jnp.float32)
        preact[span] = value
        slope = gate(value) + value * jnp.exp(-0.5 * value * value) * 0.3989422804014327
        slopes[span] = (upstream[span].astype(jnp.float32) * slope).astype(jnp.bfloat16)
    rows = hidden[:, 1 - lax.axis_index("core")].reshape(chips * feat_cols, block)
    grad = jnp.dot(rows, slopes[...], preferred_element_type=jnp.float32)
    sent[...] = grad.astype(jnp.bfloat16).reshape(sent.shape)


def rest_kernel(hidden, preact, slopes, activation, kept):
    chips, cores, feat_cols, block = hidden.shape
    rows = hidden[:, lax.axis_index("core")].reshape(chips * feat_cols, block)
    grad = jnp.dot(rows, slopes[...], preferred_element_type=jnp.float32)
    kept[...] = grad.reshape(kept.shape)
    activation[...] = (preact[...] * gate(preact[...])).astype(jnp.bfloat16)


def call_in_vmem(kernel, name, outputs, *operands):
    in_vmem = pl.BlockSpec(memory_space=pltpu.VMEM)
    return pl.pallas_call(
        kernel,
        out_shape=outputs,
        in_specs=[in_vmem] * len(operands),
        out_specs=[in_vmem] * len(outputs),
        compiler_params=pltpu.CompilerParams(vmem_limit_bytes=32 << 20),
        name=name,
    )(*operands)


def layer(hidden, weight, upstream):
    chips, cores, feat_cols, _ = hidden.shape
    grad_shape = (chips, feat_cols, weight.shape[1])
    preact, slopes, sent = call_in_vmem(
        slopes_kernel,
        "slopes",
        (
            jax.ShapeDtypeStruct(upstream.shape, jnp.float32),
            jax.ShapeDtypeStruct(upstream.shape, jnp.bfloat16),
            jax.ShapeDtypeStruct(grad_shape, jnp.bfloat16),
        ),
        hidden,
        weight,
        upstream,
    )
    received = lax.ppermute(sent, "core", [(0, 1), (1, 0)])
    activation, kept = call_in_vmem(
        rest_kernel,
        "rest",
        (
            jax.ShapeDtypeStruct(upstream.shape, jnp.bfloat16),
            jax.ShapeDtypeStruct(grad_shape, jnp.float32),
        ),
        hidden,
        preact,
        slopes,
    )
    return activation, (kept + received).astype(jnp.bfloat16)


def per_device(features, tile_rows, tile_cols, tile_masks, weight, upstream):
    peers = weight.shape[0] // features.shape[0]
    hidden = aggregate(features, tile_rows, tile_cols, tile_masks, peers)
    hidden, weight, upstream = lax.optimization_barrier((hidden, weight, upstream))
    hidden = lax.all_to_all(hidden, FEAT, 0, 0)
    hidden = hidden.reshape(peers // CORES, CORES, *hidden.shape[1:])
    activation, partial = layer(hidden, weight, upstream)
    partial = lax.all_to_all(partial, ("z", "x"), 0, 0)
    local_grad = jnp.sum(partial.astype(jnp.float32), axis=0)
    weight_grad = local_grad
    for shift in (1, 3, 2):
        pairs = [(member, member ^ shift) for member in range(N_MB)]
        weight_grad += lax.ppermute(local_grad, "mb", pairs)
    return (activation, weight_grad)


def solution(mesh):
    side = mesh.shape["feat"] // CORES
    side = int(side**0.5)
    mesh = Mesh(
        mesh.devices.reshape(mesh.shape["mb"], side, side, CORES), ("mb",) + FEAT
    )
    return jax.shard_map(
        per_device,
        mesh=mesh,
        in_specs=(
            P(FEAT, "mb"),
            P("mb"),
            P("mb"),
            P("mb", None, None),
            P(),
            P(("mb",) + FEAT, None),
        ),
        out_specs=(P(("mb",) + FEAT, None), P(FEAT, None)),
        check_vma=False,
    )
```

```python
import jax
import jax.numpy as jnp
from jax import lax
from jax.experimental import pallas as pl
from jax.experimental.pallas import tpu as pltpu
from jax.sharding import Mesh
from jax.sharding import PartitionSpec as P

NT = 16384
MB_TARGETS = ((1, 0, 3, 2), (2, 3, 1, 0), (3, 2, 0, 1))
CORES = 2
FEAT = ("z", "x", "core")
TILE = 128
CHUNK = 32
AHEAD = 3
FINISH = 8
SPAN = 256


def aggregate_kernel(
    row_index,
    col_index,
    features,
    masks,
    hidden,
    rows,
    cols,
    own,
    total,
    degree,
    picked,
    mask_buf,
    index_sem,
    self_sem,
    pick_sem,
    mask_sem,
):
    feat_cols = features.shape[0]
    chunks = mask_buf.shape[0] // CHUNK
    peers, _, block = hidden.shape

    def mask_copy(chunk):
        span = pl.ds(chunk * CHUNK, CHUNK)
        return pltpu.make_async_copy(masks.at[span], mask_buf.at[span], mask_sem.at[chunk])

    def start_pick(chunk, k):
        tile = chunk * CHUNK + k
        first = pl.multiple_of(cols[tile] * TILE, TILE)
        pltpu.make_async_copy(
            features.at[:, pl.ds(first, TILE)], picked.at[tile], pick_sem.at[chunk]
        ).start()

    fetch_rows = pltpu.make_async_copy(row_index, rows, index_sem.at[0])
    fetch_cols = pltpu.make_async_copy(col_index, cols, index_sem.at[1])

    def own_copy(part):
        span = pl.ds(part * (FINISH * block), FINISH * block)
        return pltpu.make_async_copy(features.at[:, span], own.at[:, span], self_sem.at[part])

    fetch_cols.start()
    fetch_rows.start()
    mask_copy(0).start()
    mask_copy(1).start()
    total[...] = jnp.zeros_like(total)
    degree[...] = jnp.zeros_like(degree)
    fetch_cols.wait()
    fetch_rows.wait()
    for chunk in range(AHEAD):
        if chunk > 1:
            mask_copy(chunk).start()
        for k in range(CHUNK):
            start_pick(chunk, k)
    counter = jnp.concatenate(
        [jnp.ones((16, TILE), jnp.bfloat16), jnp.zeros((16, TILE), jnp.bfloat16)], axis=1
    )

    def chunk_step(chunk, prefetch):
        span = pl.ds(chunk * CHUNK, CHUNK)
        if prefetch:
            mask_copy(chunk + AHEAD).start()
        mask_copy(chunk).wait()
        pltpu.make_async_copy(picked.at[span], picked.at[span], pick_sem.at[chunk]).wait()
        for k in range(CHUNK):
            if prefetch:
                start_pick(chunk + AHEAD, k)
            tile = chunk * CHUNK + k
            values = picked[tile]
            high = values.astype(jnp.bfloat16)
            low = (values - high.astype(jnp.float32)).astype(jnp.bfloat16)
            halves = jnp.concatenate([jnp.concatenate([high, low], axis=1), counter], axis=0)
            links = mask_buf[tile].astype(jnp.float32).astype(jnp.bfloat16).T
            sums = jnp.dot(
                halves,
                jnp.concatenate([links, links], axis=0),
                preferred_element_type=jnp.float32,
            )
            target = pl.ds(pl.multiple_of(rows[tile] * TILE, TILE), TILE)
            total[:, target] += sums[:feat_cols]
            degree[:, target] += sums[feat_cols : feat_cols + 8]

    @pl.loop(0, chunks - AHEAD)
    def _(chunk):
        chunk_step(chunk, True)

    for part in range(peers // FINISH):
        own_copy(part).start()

    @pl.loop(chunks - AHEAD, chunks)
    def _(chunk):
        chunk_step(chunk, False)

    @pl.loop(0, peers // FINISH)
    def _(step):
        own_copy(step).wait()
        for k in range(FINISH):
            peer = step * FINISH + k
            span = pl.ds(pl.multiple_of(peer * block, block), block)
            scale = 1.0 / (degree[:, span] + 1.0)
            mean = (total[:, span] + own[:, span]).reshape(feat_cols // 8, 8, block) * scale[None]
            hidden[peer] = mean.reshape(feat_cols, block).astype(jnp.bfloat16)


def aggregate(features, tile_rows, tile_cols, tile_masks, peers):
    feat_cols = features.shape[0]
    tiles = tile_masks.shape[0]
    chunks = tiles // CHUNK
    return pl.pallas_call(
        aggregate_kernel,
        out_shape=jax.ShapeDtypeStruct((peers, feat_cols, NT // peers), jnp.bfloat16),
        in_specs=[
            pl.BlockSpec(memory_space=pltpu.HBM),
            pl.BlockSpec(memory_space=pltpu.HBM),
            pl.BlockSpec(memory_space=pltpu.HBM),
            pl.BlockSpec(memory_space=pltpu.HBM),
        ],
        out_specs=pl.BlockSpec(memory_space=pltpu.VMEM),
        scratch_shapes=[
            pltpu.SMEM((tiles,), jnp.int32),
            pltpu.SMEM((tiles,), jnp.int32),
            pltpu.VMEM((feat_cols, NT), jnp.float32),
            pltpu.VMEM((feat_cols, NT), jnp.float32),
            pltpu.VMEM((8, NT), jnp.float32),
            pltpu.VMEM((tiles, feat_cols, TILE), jnp.float32),
            pltpu.VMEM((tiles, TILE, TILE), jnp.int32),
            pltpu.SemaphoreType.DMA((2,)),
            pltpu.SemaphoreType.DMA((peers // FINISH,)),
            pltpu.SemaphoreType.DMA((chunks,)),
            pltpu.SemaphoreType.DMA((chunks,)),
        ],
        compiler_params=pltpu.CompilerParams(vmem_limit_bytes=32 << 20),
        name="aggregate",
    )(
        *(
            pltpu.with_memory_space_constraint(operand, pltpu.HBM)
            for operand in (tile_rows, tile_cols, features, tile_masks)
        )
    )


def gate(preact):
    return 0.5 * (1.0 + lax.erf(preact * 0.7071067811865476))


def slopes_kernel(hidden, weight, upstream, preact, slopes, sent):
    chips, cores, feat_cols, block = hidden.shape
    other = 1 - lax.axis_index("core")
    grad = None
    for first in range(0, block, SPAN):
        span = slice(first, first + SPAN)
        for begin in range(first, first + SPAN, TILE):
            part = slice(begin, begin + TILE)
            features = hidden[:, :, :, part].reshape(chips * cores * feat_cols, TILE)
            value = jnp.dot(features.T, weight[...], preferred_element_type=jnp.float32)
            preact[part] = value
            slope = gate(value) + value * jnp.exp(-0.5 * value * value) * 0.3989422804014327
            slopes[part] = (upstream[part].astype(jnp.float32) * slope).astype(jnp.bfloat16)
        rows = hidden[:, other, :, span].reshape(chips * feat_cols, SPAN)
        term = jnp.dot(rows, slopes[span], preferred_element_type=jnp.float32)
        grad = term if grad is None else grad + term
    sent[...] = grad.astype(jnp.bfloat16).reshape(sent.shape)


def rest_kernel(hidden, preact, slopes, activation, kept):
    chips, cores, feat_cols, block = hidden.shape
    rows = hidden[:, lax.axis_index("core")].reshape(chips * feat_cols, block)
    grad = jnp.dot(rows, slopes[...], preferred_element_type=jnp.float32)
    kept[...] = grad.reshape(kept.shape)
    activation[...] = (preact[...] * gate(preact[...])).astype(jnp.bfloat16)


def call_in_vmem(kernel, name, outputs, *operands):
    in_vmem = pl.BlockSpec(memory_space=pltpu.VMEM)
    return pl.pallas_call(
        kernel,
        out_shape=outputs,
        in_specs=[in_vmem] * len(operands),
        out_specs=[in_vmem] * len(outputs),
        compiler_params=pltpu.CompilerParams(vmem_limit_bytes=32 << 20),
        name=name,
    )(*operands)


def layer(hidden, weight, upstream):
    chips, cores, feat_cols, _ = hidden.shape
    grad_shape = (chips, feat_cols, weight.shape[1])
    preact, slopes, sent = call_in_vmem(
        slopes_kernel,
        "slopes",
        (
            jax.ShapeDtypeStruct(upstream.shape, jnp.float32),
            jax.ShapeDtypeStruct(upstream.shape, jnp.bfloat16),
            jax.ShapeDtypeStruct(grad_shape, jnp.bfloat16),
        ),
        hidden,
        weight,
        upstream,
    )
    received = lax.ppermute(sent, "core", [(0, 1), (1, 0)])
    activation, kept = call_in_vmem(
        rest_kernel,
        "rest",
        (
            jax.ShapeDtypeStruct(upstream.shape, jnp.bfloat16),
            jax.ShapeDtypeStruct(grad_shape, jnp.float32),
        ),
        hidden,
        preact,
        slopes,
    )
    return activation, (kept + received).astype(jnp.bfloat16)


def per_device(features, tile_rows, tile_cols, tile_masks, weight, upstream):
    peers = weight.shape[0] // features.shape[0]
    hidden = aggregate(features, tile_rows, tile_cols, tile_masks, peers)
    hidden = lax.all_to_all(hidden, FEAT, 0, 0)
    hidden = hidden.reshape(peers // CORES, CORES, *hidden.shape[1:])
    activation, partial = layer(hidden, weight, upstream)
    partial = lax.all_to_all(partial, ("z", "x"), 0, 0)
    local_grad = jnp.sum(partial.astype(jnp.float32), axis=0)
    weight_grad = local_grad
    for targets in MB_TARGETS:
        pairs = list(enumerate(targets))
        weight_grad += lax.ppermute(local_grad, "mb", pairs)
    return (activation, weight_grad)


def solution(mesh):
    side = mesh.shape["feat"] // CORES
    side = int(side**0.5)
    mesh = Mesh(
        mesh.devices.reshape(mesh.shape["mb"], side, side, CORES), ("mb",) + FEAT
    )
    return jax.shard_map(
        per_device,
        mesh=mesh,
        in_specs=(
            P(FEAT, "mb"),
            P("mb"),
            P("mb"),
            P("mb", None, None),
            P(),
            P(("mb",) + FEAT, None),
        ),
        out_specs=(P(("mb",) + FEAT, None), P(FEAT, None)),
        check_vma=False,
    )
```

```python
import jax
import jax.numpy as jnp
from jax import lax
from jax.experimental import pallas as pl
from jax.experimental.pallas import tpu as pltpu
from jax.sharding import Mesh
from jax.sharding import PartitionSpec as P

NT = 16384
MB_TARGETS = ((1, 0, 3, 2), (2, 3, 1, 0), (3, 2, 0, 1))
CORES = 2
FEAT = ("z", "x", "core")
TILE = 128
CHUNK = 32
AHEAD = 3
FINISH = 8
SPAN = 256


def aggregate_kernel(
    row_index,
    col_index,
    features,
    masks,
    hidden,
    rows,
    cols,
    own,
    total,
    degree,
    picked,
    mask_buf,
    index_sem,
    self_sem,
    pick_sem,
    mask_sem,
):
    feat_cols = features.shape[0]
    chunks = mask_buf.shape[0] // CHUNK
    peers, _, block = hidden.shape

    def mask_copy(chunk):
        span = pl.ds(chunk * CHUNK, CHUNK)
        return pltpu.make_async_copy(masks.at[span], mask_buf.at[span], mask_sem.at[chunk])

    def start_pick(chunk, k):
        tile = chunk * CHUNK + k
        first = pl.multiple_of(cols[tile] * TILE, TILE)
        pltpu.make_async_copy(
            features.at[:, pl.ds(first, TILE)], picked.at[tile], pick_sem.at[chunk]
        ).start()

    fetch_rows = pltpu.make_async_copy(row_index, rows, index_sem.at[0])
    fetch_cols = pltpu.make_async_copy(col_index, cols, index_sem.at[1])

    def own_copy(part):
        span = pl.ds(part * (FINISH * block), FINISH * block)
        return pltpu.make_async_copy(features.at[:, span], own.at[:, span], self_sem.at[part])

    fetch_cols.start()
    fetch_rows.start()
    mask_copy(0).start()
    mask_copy(1).start()
    total[...] = jnp.zeros_like(total)
    degree[...] = jnp.zeros_like(degree)
    fetch_cols.wait()
    fetch_rows.wait()
    for chunk in range(AHEAD):
        if chunk > 1:
            mask_copy(chunk).start()
        for k in range(CHUNK):
            start_pick(chunk, k)
    counter = jnp.concatenate(
        [jnp.ones((16, TILE), jnp.bfloat16), jnp.zeros((16, TILE), jnp.bfloat16)], axis=1
    )

    def chunk_step(chunk, prefetch):
        span = pl.ds(chunk * CHUNK, CHUNK)
        if prefetch:
            mask_copy(chunk + AHEAD).start()
        mask_copy(chunk).wait()
        pltpu.make_async_copy(picked.at[span], picked.at[span], pick_sem.at[chunk]).wait()
        for k in range(CHUNK):
            if prefetch:
                start_pick(chunk + AHEAD, k)
            tile = chunk * CHUNK + k
            values = picked[tile]
            high = values.astype(jnp.bfloat16)
            low = (values - high.astype(jnp.float32)).astype(jnp.bfloat16)
            halves = jnp.concatenate([jnp.concatenate([high, low], axis=1), counter], axis=0)
            links = mask_buf[tile].astype(jnp.float32).astype(jnp.bfloat16).T
            sums = jnp.dot(
                halves,
                jnp.concatenate([links, links], axis=0),
                preferred_element_type=jnp.float32,
            )
            target = pl.ds(pl.multiple_of(rows[tile] * TILE, TILE), TILE)
            total[:, target] += sums[:feat_cols]
            degree[:, target] += sums[feat_cols : feat_cols + 8]

    @pl.loop(0, chunks - AHEAD)
    def _(chunk):
        chunk_step(chunk, True)

    for part in range(peers // FINISH):
        own_copy(part).start()

    @pl.loop(chunks - AHEAD, chunks)
    def _(chunk):
        chunk_step(chunk, False)

    @pl.loop(0, peers // FINISH)
    def _(step):
        own_copy(step).wait()
        for k in range(FINISH):
            peer = step * FINISH + k
            span = pl.ds(pl.multiple_of(peer * block, block), block)
            scale = 1.0 / (degree[:, span] + 1.0)
            mean = (total[:, span] + own[:, span]).reshape(feat_cols // 8, 8, block) * scale[None]
            hidden[peer] = mean.reshape(feat_cols, block).astype(jnp.bfloat16)


def aggregate(features, tile_rows, tile_cols, tile_masks, peers):
    feat_cols = features.shape[0]
    tiles = tile_masks.shape[0]
    chunks = tiles // CHUNK
    return pl.pallas_call(
        aggregate_kernel,
        out_shape=jax.ShapeDtypeStruct((peers, feat_cols, NT // peers), jnp.bfloat16),
        in_specs=[
            pl.BlockSpec(memory_space=pltpu.HBM),
            pl.BlockSpec(memory_space=pltpu.HBM),
            pl.BlockSpec(memory_space=pltpu.HBM),
            pl.BlockSpec(memory_space=pltpu.HBM),
        ],
        out_specs=pl.BlockSpec(memory_space=pltpu.VMEM),
        scratch_shapes=[
            pltpu.SMEM((tiles,), jnp.int32),
            pltpu.SMEM((tiles,), jnp.int32),
            pltpu.VMEM((feat_cols, NT), jnp.float32),
            pltpu.VMEM((feat_cols, NT), jnp.float32),
            pltpu.VMEM((8, NT), jnp.float32),
            pltpu.VMEM((tiles, feat_cols, TILE), jnp.float32),
            pltpu.VMEM((tiles, TILE, TILE), jnp.int32),
            pltpu.SemaphoreType.DMA((2,)),
            pltpu.SemaphoreType.DMA((peers // FINISH,)),
            pltpu.SemaphoreType.DMA((chunks,)),
            pltpu.SemaphoreType.DMA((chunks,)),
        ],
        compiler_params=pltpu.CompilerParams(vmem_limit_bytes=32 << 20),
        name="aggregate",
    )(
        *(
            pltpu.with_memory_space_constraint(operand, pltpu.HBM)
            for operand in (tile_rows, tile_cols, features, tile_masks)
        )
    )


def gate(preact):
    return 0.5 * (1.0 + lax.erf(preact * 0.7071067811865476))


def slopes_kernel(hidden, weight, upstream, preact, slopes, sent):
    chips, cores, feat_cols, block = hidden.shape
    other = 1 - lax.axis_index("core")
    grad = None
    for first in range(0, block, SPAN):
        span = slice(first, first + SPAN)
        for begin in range(first, first + SPAN, TILE):
            part = slice(begin, begin + TILE)
            features = hidden[:, :, :, part].reshape(chips * cores * feat_cols, TILE)
            value = jnp.dot(features.T, weight[...], preferred_element_type=jnp.float32)
            preact[part] = value
            slope = gate(value) + value * jnp.exp(-0.5 * value * value) * 0.3989422804014327
            slopes[part] = (upstream[part].astype(jnp.float32) * slope).astype(jnp.bfloat16)
        rows = hidden[:, other, :, span].reshape(chips * feat_cols, SPAN)
        term = jnp.dot(rows, slopes[span], preferred_element_type=jnp.float32)
        grad = term if grad is None else grad + term
    sent[...] = grad.astype(jnp.bfloat16).reshape(sent.shape)


def kept_kernel(hidden, slopes, kept):
    chips, cores, feat_cols, block = hidden.shape
    rows = hidden[:, lax.axis_index("core")].reshape(chips * feat_cols, block)
    grad = jnp.dot(rows, slopes[...], preferred_element_type=jnp.float32)
    kept[...] = grad.reshape(kept.shape)


def activation_kernel(preact, activation):
    activation[...] = (preact[...] * gate(preact[...])).astype(jnp.bfloat16)


def call_in_vmem(kernel, name, outputs, *operands):
    in_vmem = pl.BlockSpec(memory_space=pltpu.VMEM)
    return pl.pallas_call(
        kernel,
        out_shape=outputs,
        in_specs=[in_vmem] * len(operands),
        out_specs=[in_vmem] * len(outputs),
        compiler_params=pltpu.CompilerParams(vmem_limit_bytes=32 << 20),
        name=name,
    )(*operands)


def layer(hidden, weight, upstream):
    chips, cores, feat_cols, _ = hidden.shape
    grad_shape = (chips, feat_cols, weight.shape[1])
    preact, slopes, sent = call_in_vmem(
        slopes_kernel,
        "slopes",
        (
            jax.ShapeDtypeStruct(upstream.shape, jnp.float32),
            jax.ShapeDtypeStruct(upstream.shape, jnp.bfloat16),
            jax.ShapeDtypeStruct(grad_shape, jnp.bfloat16),
        ),
        hidden,
        weight,
        upstream,
    )
    received = lax.ppermute(sent, "core", [(0, 1), (1, 0)])
    (kept,) = call_in_vmem(
        kept_kernel, "kept", (jax.ShapeDtypeStruct(grad_shape, jnp.float32),), hidden, slopes
    )
    return preact, (kept + received).astype(jnp.bfloat16)


def per_device(features, tile_rows, tile_cols, tile_masks, weight, upstream):
    peers = weight.shape[0] // features.shape[0]
    hidden = aggregate(features, tile_rows, tile_cols, tile_masks, peers)
    hidden = lax.all_to_all(hidden, FEAT, 0, 0)
    hidden = hidden.reshape(peers // CORES, CORES, *hidden.shape[1:])
    preact, partial = layer(hidden, weight, upstream)
    partial = lax.all_to_all(partial, ("z", "x"), 0, 0)
    local_grad = jnp.sum(partial.astype(jnp.float32), axis=0)
    local_grad, preact = lax.optimization_barrier((local_grad, preact))
    (activation,) = call_in_vmem(
        activation_kernel,
        "activation",
        (jax.ShapeDtypeStruct(preact.shape, jnp.bfloat16),),
        preact,
    )
    weight_grad = local_grad
    for targets in MB_TARGETS:
        pairs = list(enumerate(targets))
        weight_grad += lax.ppermute(local_grad, "mb", pairs)
    return (activation, weight_grad)


def solution(mesh):
    side = mesh.shape["feat"] // CORES
    side = int(side**0.5)
    mesh = Mesh(
        mesh.devices.reshape(mesh.shape["mb"], side, side, CORES), ("mb",) + FEAT
    )
    return jax.shard_map(
        per_device,
        mesh=mesh,
        in_specs=(
            P(FEAT, "mb"),
            P("mb"),
            P("mb"),
            P("mb", None, None),
            P(),
            P(("mb",) + FEAT, None),
        ),
        out_specs=(P(("mb",) + FEAT, None), P(FEAT, None)),
        check_vma=False,
    )
```

```python
import jax
import jax.numpy as jnp
from jax import lax
from jax.experimental import pallas as pl
from jax.experimental.pallas import tpu as pltpu
from jax.sharding import Mesh
from jax.sharding import PartitionSpec as P

NT = 16384
MB_TARGETS = ((1, 0, 3, 2), (2, 3, 1, 0), (3, 2, 0, 1))
CORES = 2
FEAT = ("z", "x", "core")
TILE = 128
CHUNK = 32
AHEAD = 3
FINISH = 8
SPAN = 256


def aggregate_kernel(
    row_index,
    col_index,
    features,
    masks,
    hidden,
    rows,
    cols,
    own,
    total,
    degree,
    picked,
    mask_buf,
    index_sem,
    self_sem,
    pick_sem,
    mask_sem,
):
    feat_cols = features.shape[0]
    chunks = mask_buf.shape[0] // CHUNK
    peers, _, block = hidden.shape

    def mask_copy(chunk):
        span = pl.ds(chunk * CHUNK, CHUNK)
        return pltpu.make_async_copy(masks.at[span], mask_buf.at[span], mask_sem.at[chunk])

    def start_pick(chunk, k):
        tile = chunk * CHUNK + k
        first = pl.multiple_of(cols[tile] * TILE, TILE)
        pltpu.make_async_copy(
            features.at[:, pl.ds(first, TILE)], picked.at[tile], pick_sem.at[chunk]
        ).start()

    fetch_rows = pltpu.make_async_copy(row_index, rows, index_sem.at[0])
    fetch_cols = pltpu.make_async_copy(col_index, cols, index_sem.at[1])

    def own_copy(part):
        span = pl.ds(part * (FINISH * block), FINISH * block)
        return pltpu.make_async_copy(features.at[:, span], own.at[:, span], self_sem.at[part])

    fetch_cols.start()
    fetch_rows.start()
    mask_copy(0).start()
    mask_copy(1).start()
    total[...] = jnp.zeros_like(total)
    degree[...] = jnp.zeros_like(degree)
    fetch_cols.wait()
    fetch_rows.wait()
    for chunk in range(AHEAD):
        if chunk > 1:
            mask_copy(chunk).start()
        for k in range(CHUNK):
            start_pick(chunk, k)
    counter = jnp.concatenate(
        [jnp.ones((16, TILE), jnp.bfloat16), jnp.zeros((16, TILE), jnp.bfloat16)], axis=1
    )

    def chunk_step(chunk, prefetch):
        span = pl.ds(chunk * CHUNK, CHUNK)
        if prefetch:
            mask_copy(chunk + AHEAD).start()
        mask_copy(chunk).wait()
        pltpu.make_async_copy(picked.at[span], picked.at[span], pick_sem.at[chunk]).wait()
        for k in range(CHUNK):
            if prefetch:
                start_pick(chunk + AHEAD, k)
            tile = chunk * CHUNK + k
            values = picked[tile]
            high = values.astype(jnp.bfloat16)
            low = (values - high.astype(jnp.float32)).astype(jnp.bfloat16)
            halves = jnp.concatenate([jnp.concatenate([high, low], axis=1), counter], axis=0)
            links = mask_buf[tile].astype(jnp.float32).astype(jnp.bfloat16).T
            sums = jnp.dot(
                halves,
                jnp.concatenate([links, links], axis=0),
                preferred_element_type=jnp.float32,
            )
            target = pl.ds(pl.multiple_of(rows[tile] * TILE, TILE), TILE)
            total[:, target] += sums[:feat_cols]
            degree[:, target] += sums[feat_cols : feat_cols + 8]

    @pl.loop(0, chunks - AHEAD)
    def _(chunk):
        chunk_step(chunk, True)

    for part in range(peers // FINISH):
        own_copy(part).start()

    @pl.loop(chunks - AHEAD, chunks)
    def _(chunk):
        chunk_step(chunk, False)

    @pl.loop(0, peers // FINISH)
    def _(step):
        own_copy(step).wait()
        for k in range(FINISH):
            peer = step * FINISH + k
            span = pl.ds(pl.multiple_of(peer * block, block), block)
            scale = 1.0 / (degree[:, span] + 1.0)
            mean = (total[:, span] + own[:, span]).reshape(feat_cols // 8, 8, block) * scale[None]
            hidden[peer] = mean.reshape(feat_cols, block).astype(jnp.bfloat16)


def aggregate(features, tile_rows, tile_cols, tile_masks, peers):
    feat_cols = features.shape[0]
    tiles = tile_masks.shape[0]
    chunks = tiles // CHUNK
    return pl.pallas_call(
        aggregate_kernel,
        out_shape=jax.ShapeDtypeStruct((peers, feat_cols, NT // peers), jnp.bfloat16),
        in_specs=[
            pl.BlockSpec(memory_space=pltpu.HBM),
            pl.BlockSpec(memory_space=pltpu.HBM),
            pl.BlockSpec(memory_space=pltpu.HBM),
            pl.BlockSpec(memory_space=pltpu.HBM),
        ],
        out_specs=pl.BlockSpec(memory_space=pltpu.VMEM),
        scratch_shapes=[
            pltpu.SMEM((tiles,), jnp.int32),
            pltpu.SMEM((tiles,), jnp.int32),
            pltpu.VMEM((feat_cols, NT), jnp.float32),
            pltpu.VMEM((feat_cols, NT), jnp.float32),
            pltpu.VMEM((8, NT), jnp.float32),
            pltpu.VMEM((tiles, feat_cols, TILE), jnp.float32),
            pltpu.VMEM((tiles, TILE, TILE), jnp.int32),
            pltpu.SemaphoreType.DMA((2,)),
            pltpu.SemaphoreType.DMA((peers // FINISH,)),
            pltpu.SemaphoreType.DMA((chunks,)),
            pltpu.SemaphoreType.DMA((chunks,)),
        ],
        compiler_params=pltpu.CompilerParams(vmem_limit_bytes=32 << 20),
        name="aggregate",
    )(
        *(
            pltpu.with_memory_space_constraint(operand, pltpu.HBM)
            for operand in (tile_rows, tile_cols, features, tile_masks)
        )
    )


def gate(preact):
    return 0.5 * (1.0 + lax.erf(preact * 0.7071067811865476))


def slopes_kernel(hidden, weight, upstream, preact, slopes, sent):
    chips, cores, feat_cols, block = hidden.shape
    other = 1 - lax.axis_index("core")
    grad = None
    for first in range(0, block, SPAN):
        span = slice(first, first + SPAN)
        for begin in range(first, first + SPAN, TILE):
            part = slice(begin, begin + TILE)
            features = hidden[:, :, :, part].reshape(chips * cores * feat_cols, TILE)
            value = jnp.dot(features.T, weight[...], preferred_element_type=jnp.float32)
            preact[part] = value
            slope = gate(value) + value * jnp.exp(-0.5 * value * value) * 0.3989422804014327
            slopes[part] = (upstream[part].astype(jnp.float32) * slope).astype(jnp.bfloat16)
        rows = hidden[:, other, :, span].reshape(chips * feat_cols, SPAN)
        term = jnp.dot(rows, slopes[span], preferred_element_type=jnp.float32)
        grad = term if grad is None else grad + term
    sent[...] = grad.astype(jnp.bfloat16).reshape(sent.shape)


def kept_kernel(hidden, slopes, kept):
    chips, cores, feat_cols, block = hidden.shape
    rows = hidden[:, lax.axis_index("core")].reshape(chips * feat_cols, block)
    grad = jnp.dot(rows, slopes[...], preferred_element_type=jnp.float32)
    kept[...] = grad.reshape(kept.shape)


def activation_kernel(preact, activation):
    activation[...] = (preact[...] * gate(preact[...])).astype(jnp.bfloat16)


def call_in_vmem(kernel, name, outputs, *operands):
    in_vmem = pl.BlockSpec(memory_space=pltpu.VMEM)
    return pl.pallas_call(
        kernel,
        out_shape=outputs,
        in_specs=[in_vmem] * len(operands),
        out_specs=[in_vmem] * len(outputs),
        compiler_params=pltpu.CompilerParams(vmem_limit_bytes=32 << 20),
        name=name,
    )(*operands)


def layer(hidden, weight, upstream):
    chips, cores, feat_cols, _ = hidden.shape
    grad_shape = (chips, feat_cols, weight.shape[1])
    preact, slopes, sent = call_in_vmem(
        slopes_kernel,
        "slopes",
        (
            jax.ShapeDtypeStruct(upstream.shape, jnp.float32),
            jax.ShapeDtypeStruct(upstream.shape, jnp.bfloat16),
            jax.ShapeDtypeStruct(grad_shape, jnp.bfloat16),
        ),
        hidden,
        weight,
        upstream,
    )
    received = lax.ppermute(sent, "core", [(0, 1), (1, 0)])
    (kept,) = call_in_vmem(
        kept_kernel, "kept", (jax.ShapeDtypeStruct(grad_shape, jnp.float32),), hidden, slopes
    )
    return preact, (kept + received).astype(jnp.bfloat16)


def per_device(features, tile_rows, tile_cols, tile_masks, weight, upstream):
    peers = weight.shape[0] // features.shape[0]
    hidden = aggregate(features, tile_rows, tile_cols, tile_masks, peers)
    hidden = lax.all_to_all(hidden, FEAT, 0, 0)
    hidden = hidden.reshape(peers // CORES, CORES, *hidden.shape[1:])
    preact, partial = layer(hidden, weight, upstream)
    partial = lax.all_to_all(partial, ("z", "x"), 0, 0)
    local_grad = jnp.sum(partial.astype(jnp.float32), axis=0)
    local_grad, preact = lax.optimization_barrier((local_grad, preact))
    (activation,) = call_in_vmem(
        activation_kernel,
        "activation",
        (jax.ShapeDtypeStruct(preact.shape, jnp.bfloat16),),
        preact,
    )
    weight_grad = local_grad
    local_grad = local_grad.astype(jnp.bfloat16)
    for targets in MB_TARGETS:
        pairs = list(enumerate(targets))
        weight_grad += lax.ppermute(local_grad, "mb", pairs).astype(jnp.float32)
    return (activation, weight_grad)


def solution(mesh):
    side = mesh.shape["feat"] // CORES
    side = int(side**0.5)
    mesh = Mesh(
        mesh.devices.reshape(mesh.shape["mb"], side, side, CORES), ("mb",) + FEAT
    )
    return jax.shard_map(
        per_device,
        mesh=mesh,
        in_specs=(
            P(FEAT, "mb"),
            P("mb"),
            P("mb"),
            P("mb", None, None),
            P(),
            P(("mb",) + FEAT, None),
        ),
        out_specs=(P(("mb",) + FEAT, None), P(FEAT, None)),
        check_vma=False,
    )
```

```python
import jax
import jax.numpy as jnp
from jax import lax
from jax.experimental import pallas as pl
from jax.experimental.pallas import tpu as pltpu
from jax.sharding import Mesh
from jax.sharding import PartitionSpec as P

NT = 16384
MB_TARGETS = ((1, 0, 3, 2), (2, 3, 1, 0), (3, 2, 0, 1))
CORES = 2
FEAT = ("z", "x", "core")
TILE = 128
CHUNK = 32
AHEAD = 3
FINISH = 4
SPAN = 256


def aggregate_kernel(
    row_index,
    col_index,
    features,
    masks,
    hidden,
    rows,
    cols,
    own,
    total,
    degree,
    picked,
    mask_buf,
    index_sem,
    self_sem,
    pick_sem,
    mask_sem,
):
    feat_cols = features.shape[0]
    chunks = mask_buf.shape[0] // CHUNK
    peers, _, block = hidden.shape

    def mask_copy(chunk):
        span = pl.ds(chunk * CHUNK, CHUNK)
        return pltpu.make_async_copy(masks.at[span], mask_buf.at[span], mask_sem.at[chunk])

    def start_pick(chunk, k):
        tile = chunk * CHUNK + k
        first = pl.multiple_of(cols[tile] * TILE, TILE)
        pltpu.make_async_copy(
            features.at[:, pl.ds(first, TILE)], picked.at[tile], pick_sem.at[chunk]
        ).start()

    fetch_rows = pltpu.make_async_copy(row_index, rows, index_sem.at[0])
    fetch_cols = pltpu.make_async_copy(col_index, cols, index_sem.at[1])

    def own_copy(part):
        span = pl.ds(part * (FINISH * block), FINISH * block)
        return pltpu.make_async_copy(features.at[:, span], own.at[:, span], self_sem.at[part])

    fetch_cols.start()
    fetch_rows.start()
    mask_copy(0).start()
    mask_copy(1).start()
    total[...] = jnp.zeros_like(total)
    degree[...] = jnp.zeros_like(degree)
    fetch_cols.wait()
    fetch_rows.wait()
    for chunk in range(AHEAD):
        if chunk > 1:
            mask_copy(chunk).start()
        for k in range(CHUNK):
            start_pick(chunk, k)
    counter = jnp.concatenate(
        [jnp.ones((16, TILE), jnp.bfloat16), jnp.zeros((16, TILE), jnp.bfloat16)], axis=1
    )

    def chunk_step(chunk, prefetch):
        span = pl.ds(chunk * CHUNK, CHUNK)
        if prefetch:
            mask_copy(chunk + AHEAD).start()
        mask_copy(chunk).wait()
        pltpu.make_async_copy(picked.at[span], picked.at[span], pick_sem.at[chunk]).wait()
        for k in range(CHUNK):
            if prefetch:
                start_pick(chunk + AHEAD, k)
            tile = chunk * CHUNK + k
            values = picked[tile]
            high = values.astype(jnp.bfloat16)
            low = (values - high.astype(jnp.float32)).astype(jnp.bfloat16)
            halves = jnp.concatenate([jnp.concatenate([high, low], axis=1), counter], axis=0)
            links = mask_buf[tile].astype(jnp.float32).astype(jnp.bfloat16).T
            sums = jnp.dot(
                halves,
                jnp.concatenate([links, links], axis=0),
                preferred_element_type=jnp.float32,
            )
            target = pl.ds(pl.multiple_of(rows[tile] * TILE, TILE), TILE)
            total[:, target] += sums[:feat_cols]
            degree[:, target] += sums[feat_cols : feat_cols + 8]

    @pl.loop(0, chunks - AHEAD)
    def _(chunk):
        chunk_step(chunk, True)

    for part in range(peers // FINISH):
        own_copy(part).start()

    @pl.loop(chunks - AHEAD, chunks)
    def _(chunk):
        chunk_step(chunk, False)

    @pl.loop(0, peers // FINISH)
    def _(step):
        own_copy(step).wait()
        for k in range(FINISH):
            peer = step * FINISH + k
            span = pl.ds(pl.multiple_of(peer * block, block), block)
            scale = 1.0 / (degree[:, span] + 1.0)
            mean = (total[:, span] + own[:, span]).reshape(feat_cols // 8, 8, block) * scale[None]
            hidden[peer] = mean.reshape(feat_cols, block).astype(jnp.bfloat16)


def aggregate(features, tile_rows, tile_cols, tile_masks, peers):
    feat_cols = features.shape[0]
    tiles = tile_masks.shape[0]
    chunks = tiles // CHUNK
    return pl.pallas_call(
        aggregate_kernel,
        out_shape=jax.ShapeDtypeStruct((peers, feat_cols, NT // peers), jnp.bfloat16),
        in_specs=[
            pl.BlockSpec(memory_space=pltpu.HBM),
            pl.BlockSpec(memory_space=pltpu.HBM),
            pl.BlockSpec(memory_space=pltpu.HBM),
            pl.BlockSpec(memory_space=pltpu.HBM),
        ],
        out_specs=pl.BlockSpec(memory_space=pltpu.VMEM),
        scratch_shapes=[
            pltpu.SMEM((tiles,), jnp.int32),
            pltpu.SMEM((tiles,), jnp.int32),
            pltpu.VMEM((feat_cols, NT), jnp.float32),
            pltpu.VMEM((feat_cols, NT), jnp.float32),
            pltpu.VMEM((8, NT), jnp.float32),
            pltpu.VMEM((tiles, feat_cols, TILE), jnp.float32),
            pltpu.VMEM((tiles, TILE, TILE), jnp.int32),
            pltpu.SemaphoreType.DMA((2,)),
            pltpu.SemaphoreType.DMA((peers // FINISH,)),
            pltpu.SemaphoreType.DMA((chunks,)),
            pltpu.SemaphoreType.DMA((chunks,)),
        ],
        compiler_params=pltpu.CompilerParams(vmem_limit_bytes=32 << 20),
        name="aggregate",
    )(
        *(
            pltpu.with_memory_space_constraint(operand, pltpu.HBM)
            for operand in (tile_rows, tile_cols, features, tile_masks)
        )
    )


def gate(preact):
    return 0.5 * (1.0 + lax.erf(preact * 0.7071067811865476))


def slopes_kernel(hidden, weight, upstream, preact, slopes, sent):
    chips, cores, feat_cols, block = hidden.shape
    other = 1 - lax.axis_index("core")
    grad = None
    for first in range(0, block, SPAN):
        span = slice(first, first + SPAN)
        for begin in range(first, first + SPAN, TILE):
            part = slice(begin, begin + TILE)
            features = hidden[:, :, :, part].reshape(chips * cores * feat_cols, TILE)
            value = jnp.dot(features.T, weight[...], preferred_element_type=jnp.float32)
            preact[part] = value
            slope = gate(value) + value * jnp.exp(-0.5 * value * value) * 0.3989422804014327
            slopes[part] = (upstream[part].astype(jnp.float32) * slope).astype(jnp.bfloat16)
        rows = hidden[:, other, :, span].reshape(chips * feat_cols, SPAN)
        term = jnp.dot(rows, slopes[span], preferred_element_type=jnp.float32)
        grad = term if grad is None else grad + term
    sent[...] = grad.astype(jnp.bfloat16).reshape(sent.shape)


def kept_kernel(hidden, slopes, kept):
    chips, cores, feat_cols, block = hidden.shape
    rows = hidden[:, lax.axis_index("core")].reshape(chips * feat_cols, block)
    grad = jnp.dot(rows, slopes[...], preferred_element_type=jnp.float32)
    kept[...] = grad.reshape(kept.shape)


def activation_kernel(preact, activation):
    activation[...] = (preact[...] * gate(preact[...])).astype(jnp.bfloat16)


def call_in_vmem(kernel, name, outputs, *operands):
    in_vmem = pl.BlockSpec(memory_space=pltpu.VMEM)
    return pl.pallas_call(
        kernel,
        out_shape=outputs,
        in_specs=[in_vmem] * len(operands),
        out_specs=[in_vmem] * len(outputs),
        compiler_params=pltpu.CompilerParams(vmem_limit_bytes=32 << 20),
        name=name,
    )(*operands)


def layer(hidden, weight, upstream):
    chips, cores, feat_cols, _ = hidden.shape
    grad_shape = (chips, feat_cols, weight.shape[1])
    preact, slopes, sent = call_in_vmem(
        slopes_kernel,
        "slopes",
        (
            jax.ShapeDtypeStruct(upstream.shape, jnp.float32),
            jax.ShapeDtypeStruct(upstream.shape, jnp.bfloat16),
            jax.ShapeDtypeStruct(grad_shape, jnp.bfloat16),
        ),
        hidden,
        weight,
        upstream,
    )
    received = lax.ppermute(sent, "core", [(0, 1), (1, 0)])
    (kept,) = call_in_vmem(
        kept_kernel, "kept", (jax.ShapeDtypeStruct(grad_shape, jnp.float32),), hidden, slopes
    )
    return preact, (kept + received).astype(jnp.bfloat16)


def per_device(features, tile_rows, tile_cols, tile_masks, weight, upstream):
    peers = weight.shape[0] // features.shape[0]
    hidden = aggregate(features, tile_rows, tile_cols, tile_masks, peers)
    hidden = lax.all_to_all(hidden, FEAT, 0, 0)
    hidden = hidden.reshape(peers // CORES, CORES, *hidden.shape[1:])
    preact, partial = layer(hidden, weight, upstream)
    partial = lax.all_to_all(partial, ("z", "x"), 0, 0)
    local_grad = jnp.sum(partial.astype(jnp.float32), axis=0)
    local_grad, preact = lax.optimization_barrier((local_grad, preact))
    (activation,) = call_in_vmem(
        activation_kernel,
        "activation",
        (jax.ShapeDtypeStruct(preact.shape, jnp.bfloat16),),
        preact,
    )
    weight_grad = local_grad
    local_grad = local_grad.astype(jnp.bfloat16)
    for targets in MB_TARGETS:
        pairs = list(enumerate(targets))
        weight_grad += lax.ppermute(local_grad, "mb", pairs).astype(jnp.float32)
    return (activation, weight_grad)


def solution(mesh):
    side = mesh.shape["feat"] // CORES
    side = int(side**0.5)
    mesh = Mesh(
        mesh.devices.reshape(mesh.shape["mb"], side, side, CORES), ("mb",) + FEAT
    )
    return jax.shard_map(
        per_device,
        mesh=mesh,
        in_specs=(
            P(FEAT, "mb"),
            P("mb"),
            P("mb"),
            P("mb", None, None),
            P(),
            P(("mb",) + FEAT, None),
        ),
        out_specs=(P(("mb",) + FEAT, None), P(FEAT, None)),
        check_vma=False,
    )
```
